32 devices in a mesh: dp: 16 (over z, y, x), cls: 2 (over core).
Axes of the slice: x: 2, y: 2, z: 4, core: 2. Of those that a mesh axis runs over, the one named last changes fastest.
Arguments:
- features: bfloat16 [3072, 2048], P('dp'), may hold values from -128 to 128
- labels: int32 [3072], P('dp'), may hold values from 0 to 16383
- weight: bfloat16 [2048, 16384], P('dp', 'cls'), may hold values from -1 to 1
- noise: float32 [16, 2, 1024, 1024], P('dp', 'cls'), may hold values from -6 to 6
Outputs:
- noisy_grad: float32 [16, 2, 1024, 1024], P('dp', 'cls')
The draws below stay inside these ranges and needn't reach their ends.
All inputs are finite; a program needn't handle non-finite values.
Results may differ from the reference program's by a relative error of at most 0.0017.
Values may be sent and summed in bfloat16 or wider, within the bound.
A program may use at most 128 MiB of HBM per device.

```python
import math
import jax
import jax.numpy as jnp
import numpy as np
from jax import lax

D = 2048
CLASSES = 16384
CSPLIT = 8
TOKENS = 3072
DSPLIT = 2
DBLK = 1024
CBLK = 1024
N_DP = 16
N_CLS = 2


def draw_features(key, part):
    subkeys = jax.random.split(jax.random.fold_in(key, 11), 3)
    row_scale = jnp.exp(jax.random.uniform(subkeys[0], (TOKENS, 1), jnp.float32, math.log(0.1), math.log(10.0)))
    col_scale = jnp.exp(jax.random.uniform(subkeys[1], (1, D), jnp.float32, math.log(0.3), math.log(3.0)))
    values = row_scale * col_scale * jnp.clip(jax.random.normal(subkeys[2], (TOKENS, D), jnp.float32), -4.0, 4.0)
    return values.astype(jnp.bfloat16)


def draw_weight(key, part):
    subkeys = jax.random.split(jax.random.fold_in(key, 13), 1)
    values = jnp.clip(jax.random.normal(subkeys[0], (D, CLASSES), jnp.float32), -4.0, 4.0) / math.sqrt(D)
    return values.astype(jnp.bfloat16)


def place_ends(values, key, least, high):
    longest = values.shape.index(max(values.shape))
    spots = []
    for shift in (0, 1):
        where = [jax.random.randint(jax.random.fold_in(key, axis), (), 0, length) for axis, length in enumerate(values.shape)]
        where[longest] = (where[longest] + shift) % values.shape[longest]
        spots.append(tuple(where))
    return values.at[spots[0]].set(least).at[spots[1]].set(high)


def shard_levels(rng, shape, cuts, smallest, high):
    def one(position, shards_of):
        steps = jax.random.uniform(jax.random.fold_in(jax.random.fold_in(rng, 6), position), (shards_of,), jnp.float32, smallest / len(cuts), high / len(cuts))
        return jnp.repeat(jnp.exp(steps), shape[position] // shards_of).reshape((-1,) + (1,) * (len(shape) - position - 1))

    gain = one(*cuts[0])
    for cut in cuts[1:]:
        gain = gain * one(*cut)
    return gain


def rank_table(amount, lean):
    loads = [(1 << 20) // math.isqrt(standing ** lean) + 1 for standing in range(1, amount + 1)]
    scale = 1 + sum(loads) // (1 << 30)
    return np.cumsum(np.array([max(1, weight // scale) for weight in loads]))


def ranked_ids(own_key, dims, amount, slope):
    listing = rank_table(amount, slope)
    ticket = jax.random.randint(jax.random.fold_in(own_key, 1), dims, 0, int(listing[amount - 1]))
    grade = jnp.searchsorted(jnp.asarray(listing, jnp.int32), ticket, side="right")
    return jax.random.permutation(jax.random.fold_in(own_key, 2), amount)[grade].astype(jnp.int32)


def centred(rng, extent, deviation, bound, cuts=(), kind=jnp.bfloat16):
    entries = deviation * jax.random.normal(rng, extent, jnp.float32)
    if cuts:
        entries = entries * shard_levels(rng, extent, cuts, -0.22, 0.18)
    return jnp.clip(entries, -bound, bound).astype(kind)


def setup_inputs(seed: int = 0) -> dict:
    streams_of = jax.random.split(jax.random.key(seed), 5)
    features = draw_features(jax.random.fold_in(streams_of[4], 71), 0)
    labels = place_ends(ranked_ids(streams_of[1], (TOKENS,), CLASSES, 1), jax.random.fold_in(streams_of[1], 3), 0, CLASSES - 1).astype(jnp.int32)
    weight = draw_weight(jax.random.fold_in(streams_of[4], 71), 0)
    noise = centred(streams_of[3], (N_DP, N_CLS, DBLK, CBLK), 1.0, 6.0, ((0, 16), (1, 2)), jnp.float32)
    return {"features": features, "labels": labels, "weight": weight, "noise": noise}


CLIP_NORM = 40.0
NOISE_STD = 0.4

def reference(features, labels, weight, noise):
    block_rows = math.gcd(TOKENS, 512)
    count = TOKENS // block_rows
    feat_blocks = features.reshape(count, block_rows, D)
    label_blocks = labels.reshape(count, block_rows)

    def step_block(accum, pair):
        feat_block, label_block = pair
        logits = jnp.dot(feat_block, weight, preferred_element_type=jnp.float32)
        row_max = lax.optimization_barrier(jnp.max(logits, axis=1))
        exponent = jnp.exp(logits - row_max[:, None])
        row_total = lax.optimization_barrier(jnp.sum(exponent, axis=1))
        row_square = lax.optimization_barrier(jnp.sum(exponent * exponent, axis=1))
        label_hit = lax.broadcasted_iota(jnp.int32, logits.shape, 1) == label_block.astype(jnp.int32)[:, None]
        onehot = label_hit.astype(logits.dtype)
        picked = lax.optimization_barrier(jnp.sum(onehot * logits, axis=1))
        energy = lax.optimization_barrier(jnp.sum(jnp.square(feat_block.astype(jnp.float32)), axis=1))
        spread = row_square / (row_total * row_total) - 2.0 * jnp.exp(picked - row_max) / row_total + 1.0
        factor = CLIP_NORM * lax.rsqrt(jnp.maximum(energy * spread, CLIP_NORM * CLIP_NORM))
        softmax = exponent / row_total[:, None]
        weighted = (factor[:, None] * (softmax - onehot)).astype(jnp.bfloat16)
        accum = accum + lax.dot_general(feat_block, weighted, (((0,), (0,)), ((), ())), preferred_element_type=jnp.float32)
        return (accum, None)
    gradient, _ = lax.scan(step_block, jnp.zeros((D, CLASSES), jnp.float32), (feat_blocks, label_blocks))
    blocked = gradient.reshape(DSPLIT, DBLK, N_CLS, CSPLIT, CBLK).transpose(0, 3, 2, 1, 4).reshape(N_DP, N_CLS, DBLK, CBLK)
    return blocked + NOISE_STD * noise
```

```python
import functools

import jax
import jax.numpy as jnp
from jax import lax
from jax.experimental import pallas as pl
from jax.experimental.pallas import tpu as pltpu
from jax.sharding import PartitionSpec as P

CSPLIT = 8
CLIP_NORM = 40.0
NOISE_STD = 0.4
GATHER_LIMIT = 16 << 20
MESH = pl.DeviceIdType.MESH


def exchange_kernel(n_dp, feat_ref, weight_ref, feats_ref, wcols_ref,
                    send_sem, sib_send_sem, recv_sem, sib_recv_sem, wsend_sem, wrecv_sem, local_sem):
    me = lax.axis_index("dp")
    cls = lax.axis_index("cls")
    core = cls % 2
    sibling = cls + 1 - 2 * core
    stages = n_dp.bit_length() - 1
    rows = feat_ref.shape[0]
    half = rows // 2
    cols = wcols_ref.shape[2]

    barrier = pltpu.get_barrier_semaphore()
    for hop in range(1, n_dp):
        pl.semaphore_signal(barrier, inc=1, device_id=((me + hop) % n_dp, cls), device_id_type=MESH)
    pl.semaphore_signal(barrier, inc=1, device_id=(me, sibling), device_id_type=MESH)
    pl.semaphore_wait(barrier, n_dp)

    bit_step = [(1 << b) * (1 - 2 * ((me // (1 << b)) % 2)) for b in range(stages)]

    def stage_steps(which):
        steps = [bit_step[b] for b in range(stages - 1, 1, -1)]
        return steps + [bit_step[1] * (1 - which) + bit_step[0] * which,
                        bit_step[0] * (1 - which) + bit_step[1] * which]

    steps = stage_steps(core)
    sib_steps = stage_steps(1 - core)

    def origin(mask, table):
        spot = me
        for s in range(stages):
            if mask >> s & 1:
                spot = spot + table[s]
        return spot

    mine = pl.ds(pl.multiple_of(core * half, half), half)
    other = pl.ds(pl.multiple_of((1 - core) * half, half), half)
    sends = []

    def forward(mask, source, slot):
        first = mask.bit_length()
        for s in range(first, stages):
            copy = pltpu.make_async_remote_copy(
                src_ref=source,
                dst_ref=feats_ref.at[slot, mine],
                send_sem=send_sem.at[mask * stages + s],
                recv_sem=recv_sem.at[mask | 1 << s],
                device_id=(me + steps[s], cls),
                device_id_type=MESH,
            )
            copy.start()
            sends.append(copy)
        if mask:
            copy = pltpu.make_async_remote_copy(
                src_ref=source,
                dst_ref=feats_ref.at[slot, mine],
                send_sem=sib_send_sem.at[mask],
                recv_sem=sib_recv_sem.at[mask],
                device_id=(me, sibling),
                device_id_type=MESH,
            )
            copy.start()
            sends.append(copy)

    forward(0, feat_ref.at[mine], me)
    keep = [
        pltpu.make_async_copy(feat_ref, feats_ref.at[me], local_sem.at[0]),
        pltpu.make_async_copy(
            weight_ref.at[:, pl.ds(pl.multiple_of(me % CSPLIT * cols, cols), cols)],
            wcols_ref.at[me], local_sem.at[1]),
    ]
    for copy in keep:
        copy.start()
    for hop in range(1, n_dp):
        peer = (me + hop) % n_dp
        copy = pltpu.make_async_remote_copy(
            src_ref=weight_ref.at[:, pl.ds(pl.multiple_of(peer % CSPLIT * cols, cols), cols)],
            dst_ref=wcols_ref.at[me],
            send_sem=wsend_sem.at[hop],
            recv_sem=wrecv_sem.at[hop],
            device_id=(peer, cls),
            device_id_type=MESH,
        )
        copy.start()
        sends.append(copy)

    def arrived(ref, sem):
        pltpu.make_async_remote_copy(
            src_ref=ref, dst_ref=ref, send_sem=sem, recv_sem=sem,
            device_id=(me, sibling), device_id_type=MESH,
        ).wait_recv()

    for mask in range(1, n_dp):
        slot = origin(mask, steps)
        arrived(feats_ref.at[slot, mine], recv_sem.at[mask])
        forward(mask, feats_ref.at[slot, mine], slot)
    for mask in range(1, n_dp):
        arrived(feats_ref.at[origin(mask, sib_steps), other], sib_recv_sem.at[mask])
    for hop in range(1, n_dp):
        arrived(wcols_ref.at[(me + n_dp - hop) % n_dp], wrecv_sem.at[hop])
    for copy in keep:
        copy.wait()
    for copy in sends:
        copy.wait_send()


def exchange(features, weight, n_dp, col_block):
    stages = n_dp.bit_length() - 1
    anywhere = pl.BlockSpec(memory_space=pl.ANY)
    dma = pltpu.SemaphoreType.DMA
    return pl.pallas_call(
        functools.partial(exchange_kernel, n_dp),
        out_shape=(
            jax.ShapeDtypeStruct((n_dp,) + features.shape, features.dtype),
            jax.ShapeDtypeStruct((n_dp, weight.shape[0], col_block), weight.dtype),
        ),
        in_specs=[anywhere] * 2,
        out_specs=(anywhere, anywhere),
        scratch_shapes=[
            dma((n_dp * stages,)), dma((n_dp,)), dma((n_dp,)), dma((n_dp,)),
            dma((n_dp,)), dma((n_dp,)), dma((2,)),
        ],
        compiler_params=pltpu.CompilerParams(collective_id=0, has_side_effects=True),
    )(features, weight)


def examples_split(features, labels, weight, noise):
    tok_rows = features.shape[0]
    feature_dim = features.shape[1]
    class_shard = weight.shape[1]
    groups = lax.axis_size("dp") // CSPLIT
    row_block = feature_dim // groups
    col_block = class_shard // CSPLIT
    slot_count = groups * CSPLIT
    feature_slots = jnp.broadcast_to(
        features.reshape(tok_rows, groups, 1, row_block), (tok_rows, groups, CSPLIT, row_block)
    ).reshape(tok_rows, slot_count, row_block)
    logits = jnp.dot(
        features,
        lax.all_gather(weight, "dp", axis=0, tiled=True),
        preferred_element_type=jnp.float32,
    )
    offset = labels - lax.axis_index("cls") * class_shard
    label_hit = lax.broadcasted_iota(jnp.int32, (tok_rows, class_shard), 1) == offset[:, None]
    onehot = label_hit.astype(jnp.float32)
    local_max = jnp.max(logits, axis=1)
    exponent = jnp.exp(logits - local_max[:, None])
    row_total = jnp.sum(exponent, axis=1)
    row_square = jnp.sum(exponent * exponent, axis=1)
    picked = jnp.sum(onehot * logits, axis=1)
    global_max = lax.pmax(local_max, "cls")
    rescale = jnp.exp(local_max - global_max)
    row_total, row_square, picked = lax.psum(
        (row_total * rescale, row_square * rescale * rescale, picked), "cls"
    )
    softmax = exponent * (jnp.exp(local_max - global_max) / row_total)[:, None]
    label_prob = jnp.exp(picked - global_max) / row_total
    spread = row_square / (row_total * row_total) - 2.0 * label_prob + 1.0
    energy = jnp.sum(jnp.square(features.astype(jnp.float32)), axis=1)
    factor = CLIP_NORM * lax.rsqrt(jnp.maximum(energy * spread, CLIP_NORM * CLIP_NORM))
    weighted = (factor[:, None] * (softmax - onehot)).astype(jnp.bfloat16)
    coef_slots = jnp.broadcast_to(
        weighted.reshape(tok_rows, 1, CSPLIT, col_block), (tok_rows, groups, CSPLIT, col_block)
    ).reshape(tok_rows, slot_count, col_block)
    feature_recv, coef_recv = (
        lax.all_to_all(feature_slots, "dp", split_axis=1, concat_axis=1, tiled=True),
        lax.all_to_all(coef_slots, "dp", split_axis=1, concat_axis=1, tiled=True),
    )
    grad_block = lax.dot_general(
        feature_recv, coef_recv, (((0, 1), (0, 1)), ((), ())), preferred_element_type=jnp.float32
    )
    return (grad_block + NOISE_STD * noise[0, 0]).reshape(noise.shape)


def on_device(features, labels, weight, noise):
    n_dp = lax.axis_size("dp")
    if n_dp * features.size * features.dtype.itemsize > GATHER_LIMIT:
        return examples_split(features, labels, weight, noise)
    feature_dim = features.shape[1]
    class_shard = weight.shape[1]
    groups = n_dp // CSPLIT
    row_block = feature_dim // groups
    col_block = class_shard // CSPLIT
    me = lax.axis_index("dp")

    own_energy = jnp.sum(jnp.square(features.astype(jnp.float32)), axis=1)
    energy = lax.all_gather(own_energy, "dp", axis=0, tiled=True)
    all_labels = lax.all_gather(labels, "dp", axis=0, tiled=True)
    feats, wcols = exchange(features, weight, n_dp, col_block)
    feats = feats.reshape(-1, feature_dim)
    wcols = wcols.reshape(feature_dim, col_block)

    logits = jnp.dot(feats, wcols, preferred_element_type=jnp.float32)
    offset = all_labels - (lax.axis_index("cls") * class_shard + me % CSPLIT * col_block)
    hit = lax.broadcasted_iota(jnp.int32, logits.shape, 1) == offset[:, None]
    local_max = jnp.max(logits, axis=1)
    exponent = jnp.exp(logits - local_max[:, None])
    stats = jnp.stack([
        local_max,
        jnp.sum(exponent, axis=1),
        jnp.sum(exponent * exponent, axis=1),
        jnp.sum(jnp.where(hit, logits, 0.0), axis=1),
    ])
    gathered = lax.all_gather(stats, ("dp", "cls"), axis=0, tiled=False)
    gathered = gathered.reshape((groups, -1) + stats.shape)[0]
    row_max = jnp.max(gathered[:, 0], axis=0)
    rescale = jnp.exp(gathered[:, 0] - row_max)
    row_total = jnp.sum(gathered[:, 1] * rescale, axis=0)
    row_square = jnp.sum(gathered[:, 2] * rescale * rescale, axis=0)
    picked = jnp.sum(gathered[:, 3], axis=0)
    spread = row_square / (row_total * row_total) - 2.0 * jnp.exp(picked - row_max) / row_total + 1.0
    factor = CLIP_NORM * lax.rsqrt(jnp.maximum(energy * spread, CLIP_NORM * CLIP_NORM))
    scale = jnp.exp(local_max - row_max) / row_total
    coef = (factor[:, None] * (exponent * scale[:, None] - hit.astype(jnp.float32))).astype(jnp.bfloat16)
    feat_rows = lax.dynamic_slice_in_dim(feats, me // CSPLIT * row_block, row_block, axis=1)
    grad = lax.dot_general(feat_rows, coef, (((0,), (0,)), ((), ())), preferred_element_type=jnp.float32)
    return (grad + NOISE_STD * noise[0, 0]).reshape(noise.shape)


def solution(mesh):
    placed = (P("dp", None), P("dp"), P("dp", "cls"), P("dp", "cls", None, None))
    return jax.shard_map(
        on_device, mesh=mesh, in_specs=placed, out_specs=P("dp", "cls", None, None), check_vma=False
    )
```

```python
import functools

import jax
import jax.numpy as jnp
from jax import lax
from jax.experimental import pallas as pl
from jax.experimental.pallas import tpu as pltpu
from jax.sharding import PartitionSpec as P

CSPLIT = 8
CLIP_NORM = 40.0
NOISE_STD = 0.4
GATHER_LIMIT = 16 << 20
MESH = pl.DeviceIdType.MESH


def exchange_kernel(n_dp, feat_ref, weight_ref, side_ref, feats_ref, wcols_ref, sides_ref,
                    send_sem, sib_send_sem, recv_sem, sib_recv_sem, wsend_sem, wrecv_sem, ssend_sem, srecv_sem, local_sem):
    me = lax.axis_index("dp")
    cls = lax.axis_index("cls")
    core = cls % 2
    sibling = cls + 1 - 2 * core
    stages = n_dp.bit_length() - 1
    rows = feat_ref.shape[0]
    half = rows // 2
    cols = wcols_ref.shape[2]

    barrier = pltpu.get_barrier_semaphore()
    for hop in range(1, n_dp):
        pl.semaphore_signal(barrier, inc=1, device_id=((me + hop) % n_dp, cls), device_id_type=MESH)
    pl.semaphore_signal(barrier, inc=1, device_id=(me, sibling), device_id_type=MESH)
    pl.semaphore_wait(barrier, n_dp)

    bit_step = [(1 << b) * (1 - 2 * ((me // (1 << b)) % 2)) for b in range(stages)]

    def stage_steps(which):
        steps = [bit_step[b] for b in range(stages - 1, 1, -1)]
        return steps + [bit_step[1] * (1 - which) + bit_step[0] * which,
                        bit_step[0] * (1 - which) + bit_step[1] * which]

    steps = stage_steps(core)
    sib_steps = stage_steps(1 - core)

    def origin(mask, table):
        spot = me
        for s in range(stages):
            if mask >> s & 1:
                spot = spot + table[s]
        return spot

    mine = pl.ds(pl.multiple_of(core * half, half), half)
    other = pl.ds(pl.multiple_of((1 - core) * half, half), half)
    sends = []

    def forward(mask, source, slot):
        first = mask.bit_length()
        for s in range(first, stages):
            copy = pltpu.make_async_remote_copy(
                src_ref=source,
                dst_ref=feats_ref.at[slot, mine],
                send_sem=send_sem.at[mask * stages + s],
                recv_sem=recv_sem.at[mask | 1 << s],
                device_id=(me + steps[s], cls),
                device_id_type=MESH,
            )
            copy.start()
            sends.append(copy)
        if mask:
            copy = pltpu.make_async_remote_copy(
                src_ref=source,
                dst_ref=feats_ref.at[slot, mine],
                send_sem=sib_send_sem.at[mask],
                recv_sem=sib_recv_sem.at[mask],
                device_id=(me, sibling),
                device_id_type=MESH,
            )
            copy.start()
            sends.append(copy)

    forward(0, feat_ref.at[mine], me)
    keep = [
        pltpu.make_async_copy(feat_ref, feats_ref.at[me], local_sem.at[0]),
        pltpu.make_async_copy(
            weight_ref.at[:, pl.ds(pl.multiple_of(me % CSPLIT * cols, cols), cols)],
            wcols_ref.at[me], local_sem.at[1]),
        pltpu.make_async_copy(side_ref, sides_ref.at[me], local_sem.at[2]),
    ]
    for copy in keep:
        copy.start()
    for hop in range(1, n_dp):
        peer = (me + hop) % n_dp
        copy = pltpu.make_async_remote_copy(
            src_ref=weight_ref.at[:, pl.ds(pl.multiple_of(peer % CSPLIT * cols, cols), cols)],
            dst_ref=wcols_ref.at[me],
            send_sem=wsend_sem.at[hop],
            recv_sem=wrecv_sem.at[hop],
            device_id=(peer, cls),
            device_id_type=MESH,
        )
        copy.start()
        sends.append(copy)
        copy = pltpu.make_async_remote_copy(
            src_ref=side_ref,
            dst_ref=sides_ref.at[me],
            send_sem=ssend_sem.at[hop],
            recv_sem=srecv_sem.at[hop],
            device_id=(peer, cls),
            device_id_type=MESH,
        )
        copy.start()
        sends.append(copy)

    def arrived(ref, sem):
        pltpu.make_async_remote_copy(
            src_ref=ref, dst_ref=ref, send_sem=sem, recv_sem=sem,
            device_id=(me, sibling), device_id_type=MESH,
        ).wait_recv()

    for mask in range(1, n_dp):
        slot = origin(mask, steps)
        arrived(feats_ref.at[slot, mine], recv_sem.at[mask])
        forward(mask, feats_ref.at[slot, mine], slot)
    for mask in range(1, n_dp):
        arrived(feats_ref.at[origin(mask, sib_steps), other], sib_recv_sem.at[mask])
    for hop in range(1, n_dp):
        arrived(wcols_ref.at[(me + n_dp - hop) % n_dp], wrecv_sem.at[hop])
        arrived(sides_ref.at[(me + n_dp - hop) % n_dp], srecv_sem.at[hop])
    for copy in keep:
        copy.wait()
    for copy in sends:
        copy.wait_send()


def exchange(features, weight, side, n_dp, col_block):
    stages = n_dp.bit_length() - 1
    anywhere = pl.BlockSpec(memory_space=pl.ANY)
    dma = pltpu.SemaphoreType.DMA
    return pl.pallas_call(
        functools.partial(exchange_kernel, n_dp),
        out_shape=(
            jax.ShapeDtypeStruct((n_dp,) + features.shape, features.dtype),
            jax.ShapeDtypeStruct((n_dp, weight.shape[0], col_block), weight.dtype),
            jax.ShapeDtypeStruct((n_dp,) + side.shape, side.dtype),
        ),
        in_specs=[anywhere] * 3,
        out_specs=(anywhere,) * 3,
        scratch_shapes=[
            dma((n_dp * stages,)), dma((n_dp,)), dma((n_dp,)), dma((n_dp,)),
            dma((n_dp,)), dma((n_dp,)), dma((n_dp,)), dma((n_dp,)), dma((3,)),
        ],
        compiler_params=pltpu.CompilerParams(collective_id=0, has_side_effects=True),
    )(features, weight, side)


def stats_kernel(n_cls, stats_ref, all_ref, send_sem, recv_sem):
    me = lax.axis_index("dp")
    cls = lax.axis_index("cls")
    first = me // CSPLIT * CSPLIT
    count = CSPLIT * n_cls
    place = me % CSPLIT * n_cls + cls

    def peer(hop):
        spot = (place + hop) % count
        return (first + spot // n_cls, spot % n_cls)

    barrier = pltpu.get_barrier_semaphore()
    for hop in range(1, count):
        pl.semaphore_signal(barrier, inc=1, device_id=peer(hop), device_id_type=MESH)
    pl.semaphore_wait(barrier, count - 1)
    copies = []
    for hop in range(1, count):
        copy = pltpu.make_async_remote_copy(
            src_ref=stats_ref,
            dst_ref=all_ref.at[place],
            send_sem=send_sem.at[hop],
            recv_sem=recv_sem.at[hop],
            device_id=peer(hop),
            device_id_type=MESH,
        )
        copy.start()
        copies.append(copy)
    all_ref[pl.ds(place, 1)] = stats_ref[...][None]
    for hop in range(1, count):
        spot = all_ref.at[(place + count - hop) % count]
        pltpu.make_async_remote_copy(
            src_ref=spot, dst_ref=spot, send_sem=send_sem.at[hop], recv_sem=recv_sem.at[hop],
            device_id=peer(hop), device_id_type=MESH,
        ).wait_recv()
    for copy in copies:
        copy.wait_send()


def gather_stats(stats, n_cls):
    count = CSPLIT * n_cls
    inside = pl.BlockSpec(memory_space=pltpu.VMEM)
    return pl.pallas_call(
        functools.partial(stats_kernel, n_cls),
        out_shape=jax.ShapeDtypeStruct((count,) + stats.shape, stats.dtype),
        in_specs=[inside],
        out_specs=inside,
        scratch_shapes=[pltpu.SemaphoreType.DMA((count,)), pltpu.SemaphoreType.DMA((count,))],
        compiler_params=pltpu.CompilerParams(collective_id=1, has_side_effects=True),
    )(stats)


def examples_split(features, labels, weight, noise):
    tok_rows = features.shape[0]
    feature_dim = features.shape[1]
    class_shard = weight.shape[1]
    groups = lax.axis_size("dp") // CSPLIT
    row_block = feature_dim // groups
    col_block = class_shard // CSPLIT
    slot_count = groups * CSPLIT
    feature_slots = jnp.broadcast_to(
        features.reshape(tok_rows, groups, 1, row_block), (tok_rows, groups, CSPLIT, row_block)
    ).reshape(tok_rows, slot_count, row_block)
    logits = jnp.dot(
        features,
        lax.all_gather(weight, "dp", axis=0, tiled=True),
        preferred_element_type=jnp.float32,
    )
    offset = labels - lax.axis_index("cls") * class_shard
    label_hit = lax.broadcasted_iota(jnp.int32, (tok_rows, class_shard), 1) == offset[:, None]
    onehot = label_hit.astype(jnp.float32)
    local_max = jnp.max(logits, axis=1)
    exponent = jnp.exp(logits - local_max[:, None])
    row_total = jnp.sum(exponent, axis=1)
    row_square = jnp.sum(exponent * exponent, axis=1)
    picked = jnp.sum(onehot * logits, axis=1)
    global_max = lax.pmax(local_max, "cls")
    rescale = jnp.exp(local_max - global_max)
    row_total, row_square, picked = lax.psum(
        (row_total * rescale, row_square * rescale * rescale, picked), "cls"
    )
    softmax = exponent * (jnp.exp(local_max - global_max) / row_total)[:, None]
    label_prob = jnp.exp(picked - global_max) / row_total
    spread = row_square / (row_total * row_total) - 2.0 * label_prob + 1.0
    energy = jnp.sum(jnp.square(features.astype(jnp.float32)), axis=1)
    factor = CLIP_NORM * lax.rsqrt(jnp.maximum(energy * spread, CLIP_NORM * CLIP_NORM))
    weighted = (factor[:, None] * (softmax - onehot)).astype(jnp.bfloat16)
    coef_slots = jnp.broadcast_to(
        weighted.reshape(tok_rows, 1, CSPLIT, col_block), (tok_rows, groups, CSPLIT, col_block)
    ).reshape(tok_rows, slot_count, col_block)
    feature_recv, coef_recv = (
        lax.all_to_all(feature_slots, "dp", split_axis=1, concat_axis=1, tiled=True),
        lax.all_to_all(coef_slots, "dp", split_axis=1, concat_axis=1, tiled=True),
    )
    grad_block = lax.dot_general(
        feature_recv, coef_recv, (((0, 1), (0, 1)), ((), ())), preferred_element_type=jnp.float32
    )
    return (grad_block + NOISE_STD * noise[0, 0]).reshape(noise.shape)


def on_device(features, labels, weight, noise):
    n_dp = lax.axis_size("dp")
    if n_dp * features.size * features.dtype.itemsize > GATHER_LIMIT:
        return examples_split(features, labels, weight, noise)
    feature_dim = features.shape[1]
    class_shard = weight.shape[1]
    groups = n_dp // CSPLIT
    row_block = feature_dim // groups
    col_block = class_shard // CSPLIT
    me = lax.axis_index("dp")

    own_energy = jnp.sum(jnp.square(features.astype(jnp.float32)), axis=1)
    side = jnp.stack([labels.astype(jnp.float32), own_energy])
    feats, wcols, sides = exchange(features, weight, side, n_dp, col_block)
    all_labels = sides[:, 0].reshape(-1).astype(jnp.int32)
    energy = sides[:, 1].reshape(-1)
    feats = feats.reshape(-1, feature_dim)
    wcols = wcols.reshape(feature_dim, col_block)

    logits = jnp.dot(feats, wcols, preferred_element_type=jnp.float32)
    offset = all_labels - (lax.axis_index("cls") * class_shard + me % CSPLIT * col_block)
    hit = lax.broadcasted_iota(jnp.int32, logits.shape, 1) == offset[:, None]
    local_max = jnp.max(logits, axis=1)
    exponent = jnp.exp(logits - local_max[:, None])
    stats = jnp.stack([
        local_max,
        jnp.sum(exponent, axis=1),
        jnp.sum(exponent * exponent, axis=1),
        jnp.sum(jnp.where(hit, logits, 0.0), axis=1),
    ])
    gathered = gather_stats(stats, lax.axis_size("cls"))
    row_max = jnp.max(gathered[:, 0], axis=0)
    rescale = jnp.exp(gathered[:, 0] - row_max)
    row_total = jnp.sum(gathered[:, 1] * rescale, axis=0)
    row_square = jnp.sum(gathered[:, 2] * rescale * rescale, axis=0)
    picked = jnp.sum(gathered[:, 3], axis=0)
    spread = row_square / (row_total * row_total) - 2.0 * jnp.exp(picked - row_max) / row_total + 1.0
    factor = CLIP_NORM * lax.rsqrt(jnp.maximum(energy * spread, CLIP_NORM * CLIP_NORM))
    scale = jnp.exp(local_max - row_max) / row_total
    coef = (factor[:, None] * (exponent * scale[:, None] - hit.astype(jnp.float32))).astype(jnp.bfloat16)
    feat_rows = lax.dynamic_slice_in_dim(feats, me // CSPLIT * row_block, row_block, axis=1)
    grad = lax.dot_general(feat_rows, coef, (((0,), (0,)), ((), ())), preferred_element_type=jnp.float32)
    return (grad + NOISE_STD * noise[0, 0]).reshape(noise.shape)


def solution(mesh):
    placed = (P("dp", None), P("dp"), P("dp", "cls"), P("dp", "cls", None, None))
    return jax.shard_map(
        on_device, mesh=mesh, in_specs=placed, out_specs=P("dp", "cls", None, None), check_vma=False
    )
```

```python
import functools

import jax
import jax.numpy as jnp
from jax import lax
from jax.experimental import pallas as pl
from jax.experimental.pallas import tpu as pltpu
from jax.sharding import PartitionSpec as P

CSPLIT = 8
CLIP_NORM = 40.0
NOISE_STD = 0.4
GATHER_LIMIT = 16 << 20
CHUNKS = 4
BLOCKS_PER_DOT = 4
MESH = pl.DeviceIdType.MESH


def head_kernel(n_dp, n_cls, feat_ref, weight_ref, side_ref, rows_ref, coef_ref,
                feats, wcols, exps, coefs, sides, lanes, labels, stats, all_stats, maxima, energies, scales,
                send_sem, sib_send_sem, recv_sem, sib_recv_sem, wsend_sem, wrecv_sem,
                ssend_sem, srecv_sem, tsend_sem, trecv_sem, local_sem, rows_sem, coef_sem):
    me = lax.axis_index("dp")
    cls = lax.axis_index("cls")
    core = cls % 2
    sibling = cls + 1 - 2 * core
    stages = n_dp.bit_length() - 1
    rows, depth = feat_ref.shape
    half = rows // 2
    chunks, _, depth_block, width = wcols.shape
    cols = chunks * width
    padded = lanes.shape[1]
    row_block = rows_ref.shape[2]
    per = BLOCKS_PER_DOT
    count = CSPLIT * n_cls
    place = me % CSPLIT * n_cls + cls

    def group_peer(hop):
        spot = (place + hop) % count
        return (me // CSPLIT * CSPLIT + spot // n_cls, spot % n_cls)

    barrier = pltpu.get_barrier_semaphore()
    for hop in range(1, n_dp):
        pl.semaphore_signal(barrier, inc=1, device_id=((me + hop) % n_dp, cls), device_id_type=MESH)
    for hop in range(1, count):
        pl.semaphore_signal(barrier, inc=1, device_id=group_peer(hop), device_id_type=MESH)
    pl.semaphore_wait(barrier, n_dp - 1 + count - 1)

    bit_step = [(1 << b) * (1 - 2 * ((me // (1 << b)) % 2)) for b in range(stages)]

    def stage_steps(which):
        table = [bit_step[b] for b in range(stages - 1, 1, -1)]
        return table + [bit_step[1] * (1 - which) + bit_step[0] * which,
                        bit_step[0] * (1 - which) + bit_step[1] * which]

    steps = stage_steps(core)
    sib_steps = stage_steps(1 - core)

    def origin(mask, table):
        spot = me
        for s in range(stages):
            if mask >> s & 1:
                spot = spot + table[s]
        return spot

    mine = pl.ds(pl.multiple_of(core * half, half), half)
    other = pl.ds(pl.multiple_of((1 - core) * half, half), half)
    sends = []

    def push(source, target, out_sem, in_sem, device):
        copy = pltpu.make_async_remote_copy(
            src_ref=source, dst_ref=target, send_sem=out_sem, recv_sem=in_sem,
            device_id=device, device_id_type=MESH,
        )
        copy.start()
        sends.append(copy)

    def arrived(ref, sem):
        pltpu.make_async_remote_copy(
            src_ref=ref, dst_ref=ref, send_sem=sem, recv_sem=sem,
            device_id=(me, sibling), device_id_type=MESH,
        ).wait_recv()

    def forward(mask, source, slot):
        for s in range(mask.bit_length(), stages):
            push(source, feats.at[slot, mine], send_sem.at[mask * stages + s],
                 recv_sem.at[mask | 1 << s], (me + steps[s], cls))
        if mask:
            push(source, feats.at[slot, mine], sib_send_sem.at[mask], sib_recv_sem.at[mask], (me, sibling))

    def send_chunk(c):
        for hop in range(1, n_dp):
            peer = (me + hop) % n_dp
            first = pl.multiple_of(peer % CSPLIT * cols + c * width, width)
            push(weight_ref.at[:, pl.ds(first, width)], wcols.at[c, me],
                 wsend_sem.at[c * n_dp + hop], wrecv_sem.at[c * n_dp + hop], (peer, cls))

    forward(0, feat_ref.at[mine], me)
    keep = [
        pltpu.make_async_copy(feat_ref, feats.at[me], local_sem.at[0]),
        pltpu.make_async_copy(side_ref, sides.at[me], local_sem.at[1]),
    ] + [
        pltpu.make_async_copy(
            weight_ref.at[:, pl.ds(pl.multiple_of(me % CSPLIT * cols + c * width, width), width)],
            wcols.at[c, me], local_sem.at[2 + c])
        for c in range(chunks)
    ]
    for copy in keep:
        copy.start()
    for hop in range(1, n_dp):
        push(side_ref, sides.at[me], ssend_sem.at[hop], srecv_sem.at[hop], ((me + hop) % n_dp, cls))
    for c in range(chunks):
        send_chunk(c)

    for hop in range(1, n_dp):
        arrived(sides.at[(me + n_dp - hop) % n_dp], srecv_sem.at[hop])
    for copy in keep:
        copy.wait()
    fill = jnp.zeros((128 - sides.shape[1], padded), jnp.float32)
    lanes[...] = jnp.zeros_like(lanes)

    def spread_labels(i, carry):
        labels[i] = jnp.concatenate([sides[i], fill], axis=0).T
        return carry

    lax.fori_loop(0, n_dp, spread_labels, 0)
    for i in range(n_dp):
        energies[i:i + 1, :] = sides[i, 1:2, :]

    for mask in range(1, n_dp):
        slot = origin(mask, steps)
        arrived(feats.at[slot, mine], recv_sem.at[mask])
        forward(mask, feats.at[slot, mine], slot)
    for mask in range(1, n_dp):
        arrived(feats.at[origin(mask, sib_steps), other], sib_recv_sem.at[mask])

    first_row = pl.multiple_of(me // CSPLIT * row_block, row_block)
    row_copies = [
        pltpu.make_async_copy(feats.at[i, :, pl.ds(first_row, row_block)], rows_ref.at[i], rows_sem.at[i])
        for i in range(n_dp)
    ]
    for copy in row_copies:
        copy.start()

    base = cls * (CSPLIT * cols) + me % CSPLIT * cols

    def hits(block_labels, c, shape):
        offset = block_labels.astype(jnp.int32) - (base + c * width)
        return lax.broadcasted_iota(jnp.int32, shape, 1) == offset

    def chunk_body(c, carry):
        for hop in range(1, n_dp):
            arrived(wcols.at[c, (me + n_dp - hop) % n_dp], wrecv_sem.at[c * n_dp + hop])

        def group_body(g, inner):
            blocks = pl.ds(g * per, per)
            logits = jnp.dot(
                feats[blocks].reshape(per * rows, depth), wcols[c].reshape(depth, width),
                preferred_element_type=jnp.float32)
            hit = hits(labels[blocks, 0:rows, 0:1].reshape(per * rows, 1), c, logits.shape)
            top = jnp.max(logits, axis=1, keepdims=True)
            exponent = jnp.exp(logits - top)
            total = jnp.sum(exponent, axis=1, keepdims=True)
            square = jnp.sum(exponent * exponent, axis=1, keepdims=True)
            picked = jnp.sum(jnp.where(hit, logits, 0.0), axis=1, keepdims=True)
            exps[c, blocks] = exponent.reshape(per, rows, width)
            held = lanes[blocks, 0:rows, :].reshape(per * rows, 128)
            lane = lax.broadcasted_iota(jnp.int32, held.shape, 1) - 4 * c
            held = jnp.where(lane == 0, top, held)
            held = jnp.where(lane == 1, total, held)
            held = jnp.where(lane == 2, square, held)
            held = jnp.where(lane == 3, picked, held)
            lanes[blocks, 0:rows, :] = held.reshape(per, rows, 128)
            return inner

        return lax.fori_loop(0, n_dp // per, group_body, carry)

    lax.fori_loop(0, chunks, chunk_body, 0)

    for i in range(n_dp):
        turned = lanes[i].T
        tops = [turned[4 * c:4 * c + 1] for c in range(chunks)]
        top = functools.reduce(jnp.maximum, tops)
        fades = [jnp.exp(t - top) for t in tops]
        stats[0, i:i + 1, :] = top
        stats[1, i:i + 1, :] = sum(turned[4 * c + 1:4 * c + 2] * fades[c] for c in range(chunks))
        stats[2, i:i + 1, :] = sum(turned[4 * c + 2:4 * c + 3] * fades[c] * fades[c] for c in range(chunks))
        stats[3, i:i + 1, :] = sum(turned[4 * c + 3:4 * c + 4] for c in range(chunks))
        for c in range(chunks):
            maxima[c, i:i + 1, :] = tops[c]

    for hop in range(1, count):
        push(stats, all_stats.at[place], tsend_sem.at[hop], trecv_sem.at[hop], group_peer(hop))
    all_stats[pl.ds(place, 1)] = stats[...][None]
    for hop in range(1, count):
        arrived(all_stats.at[(place + count - hop) % count], trecv_sem.at[hop])

    row_max = all_stats[0, 0]
    for d in range(1, count):
        row_max = jnp.maximum(row_max, all_stats[d, 0])
    row_total = jnp.zeros_like(row_max)
    row_square = jnp.zeros_like(row_max)
    picked = jnp.zeros_like(row_max)
    for d in range(count):
        fade = jnp.exp(all_stats[d, 0] - row_max)
        row_total = row_total + all_stats[d, 1] * fade
        row_square = row_square + all_stats[d, 2] * fade * fade
        picked = picked + all_stats[d, 3]
    spread = row_square / (row_total * row_total) - 2.0 * jnp.exp(picked - row_max) / row_total + 1.0
    factor = CLIP_NORM * lax.rsqrt(jnp.maximum(energies[...] * spread, CLIP_NORM * CLIP_NORM))
    scales[chunks] = factor
    for c in range(chunks):
        scales[c] = factor * (jnp.exp(maxima[c] - row_max) / row_total)
    for i in range(n_dp):
        for c in range(chunks + 1):
            sides[i, c:c + 1, :] = scales[c, i:i + 1, :]

    def coef_copy(i):
        return pltpu.make_async_copy(coefs.at[i], coef_ref.at[i], coef_sem.at[i])

    def coef_body(i, carry):
        columns = jnp.concatenate([sides[i], fill], axis=0).T[0:rows]
        block_labels = labels[i, 0:rows, 0:1]
        for c in range(chunks):
            hit = hits(block_labels, c, (rows, width))
            value = exps[c, i] * columns[:, c:c + 1] - jnp.where(hit, columns[:, chunks:chunks + 1], 0.0)
            coefs[i, :, c * width:(c + 1) * width] = value.astype(coefs.dtype)
        coef_copy(i).start()
        return carry

    lax.fori_loop(0, n_dp, coef_body, 0)
    for i in range(n_dp):
        coef_copy(i).wait()
        row_copies[i].wait()
    for copy in sends:
        copy.wait_send()


def head(features, weight, side, n_dp, n_cls, row_block, col_block):
    stages = n_dp.bit_length() - 1
    rows, depth = features.shape
    padded = side.shape[1]
    count = CSPLIT * n_cls
    width = col_block // CHUNKS
    anywhere = pl.BlockSpec(memory_space=pl.ANY)
    dma = pltpu.SemaphoreType.DMA
    f32 = jnp.float32
    return pl.pallas_call(
        functools.partial(head_kernel, n_dp, n_cls),
        out_shape=(
            jax.ShapeDtypeStruct((n_dp, rows, row_block), features.dtype),
            jax.ShapeDtypeStruct((n_dp, rows, col_block), jnp.bfloat16),
        ),
        in_specs=[anywhere] * 3,
        out_specs=(anywhere,) * 2,
        scratch_shapes=[
            pltpu.VMEM((n_dp, rows, depth), features.dtype),
            pltpu.VMEM((CHUNKS, n_dp, weight.shape[0], width), weight.dtype),
            pltpu.VMEM((CHUNKS, n_dp, rows, width), f32),
            pltpu.VMEM((n_dp, rows, col_block), jnp.bfloat16),
            pltpu.VMEM((n_dp,) + side.shape, f32),
            pltpu.VMEM((n_dp, padded, 128), f32),
            pltpu.VMEM((n_dp, padded, 128), f32),
            pltpu.VMEM((4, n_dp, padded), f32),
            pltpu.VMEM((count, 4, n_dp, padded), f32),
            pltpu.VMEM((CHUNKS, n_dp, padded), f32),
            pltpu.VMEM((n_dp, padded), f32),
            pltpu.VMEM((CHUNKS + 1, n_dp, padded), f32),
            dma((n_dp * stages,)), dma((n_dp,)), dma((n_dp,)), dma((n_dp,)),
            dma((CHUNKS * n_dp,)), dma((CHUNKS * n_dp,)),
            dma((n_dp,)), dma((n_dp,)), dma((count,)), dma((count,)),
            dma((2 + CHUNKS,)), dma((n_dp,)), dma((n_dp,)),
        ],
        compiler_params=pltpu.CompilerParams(
            collective_id=0, has_side_effects=True, vmem_limit_bytes=60 << 20),
    )(features, weight, side)


def examples_split(features, labels, weight, noise):
    tok_rows = features.shape[0]
    feature_dim = features.shape[1]
    class_shard = weight.shape[1]
    groups = lax.axis_size("dp") // CSPLIT
    row_block = feature_dim // groups
    col_block = class_shard // CSPLIT
    slot_count = groups * CSPLIT
    feature_slots = jnp.broadcast_to(
        features.reshape(tok_rows, groups, 1, row_block), (tok_rows, groups, CSPLIT, row_block)
    ).reshape(tok_rows, slot_count, row_block)
    logits = jnp.dot(
        features,
        lax.all_gather(weight, "dp", axis=0, tiled=True),
        preferred_element_type=jnp.float32,
    )
    offset = labels - lax.axis_index("cls") * class_shard
    label_hit = lax.broadcasted_iota(jnp.int32, (tok_rows, class_shard), 1) == offset[:, None]
    onehot = label_hit.astype(jnp.float32)
    local_max = jnp.max(logits, axis=1)
    exponent = jnp.exp(logits - local_max[:, None])
    row_total = jnp.sum(exponent, axis=1)
    row_square = jnp.sum(exponent * exponent, axis=1)
    picked = jnp.sum(onehot * logits, axis=1)
    global_max = lax.pmax(local_max, "cls")
    rescale = jnp.exp(local_max - global_max)
    row_total, row_square, picked = lax.psum(
        (row_total * rescale, row_square * rescale * rescale, picked), "cls"
    )
    softmax = exponent * (jnp.exp(local_max - global_max) / row_total)[:, None]
    label_prob = jnp.exp(picked - global_max) / row_total
    spread = row_square / (row_total * row_total) - 2.0 * label_prob + 1.0
    energy = jnp.sum(jnp.square(features.astype(jnp.float32)), axis=1)
    factor = CLIP_NORM * lax.rsqrt(jnp.maximum(energy * spread, CLIP_NORM * CLIP_NORM))
    weighted = (factor[:, None] * (softmax - onehot)).astype(jnp.bfloat16)
    coef_slots = jnp.broadcast_to(
        weighted.reshape(tok_rows, 1, CSPLIT, col_block), (tok_rows, groups, CSPLIT, col_block)
    ).reshape(tok_rows, slot_count, col_block)
    feature_recv, coef_recv = (
        lax.all_to_all(feature_slots, "dp", split_axis=1, concat_axis=1, tiled=True),
        lax.all_to_all(coef_slots, "dp", split_axis=1, concat_axis=1, tiled=True),
    )
    grad_block = lax.dot_general(
        feature_recv, coef_recv, (((0, 1), (0, 1)), ((), ())), preferred_element_type=jnp.float32
    )
    return (grad_block + NOISE_STD * noise[0, 0]).reshape(noise.shape)


def on_device(features, labels, weight, noise):
    n_dp = lax.axis_size("dp")
    if n_dp * features.size * features.dtype.itemsize > GATHER_LIMIT:
        return examples_split(features, labels, weight, noise)
    feature_dim = features.shape[1]
    class_shard = weight.shape[1]
    groups = n_dp // CSPLIT
    row_block = feature_dim // groups
    col_block = class_shard // CSPLIT
    padded = -(-features.shape[0] // 128) * 128
    own_energy = jnp.sum(jnp.square(features.astype(jnp.float32)), axis=1)
    side = jnp.pad(
        jnp.stack([labels.astype(jnp.float32), own_energy]), ((0, 6), (0, padded - features.shape[0])))
    rows, coef = head(features, weight, side, n_dp, lax.axis_size("cls"), row_block, col_block)
    grad = lax.dot_general(rows, coef, (((0, 1), (0, 1)), ((), ())), preferred_element_type=jnp.float32)
    return (grad + NOISE_STD * noise[0, 0]).reshape(noise.shape)


def solution(mesh):
    placed = (P("dp", None), P("dp"), P("dp", "cls"), P("dp", "cls", None, None))
    return jax.shard_map(
        on_device, mesh=mesh, in_specs=placed, out_specs=P("dp", "cls", None, None), check_vma=False
    )
```

```python
import functools

import jax
import jax.numpy as jnp
from jax import lax
from jax.experimental import pallas as pl
from jax.experimental.pallas import tpu as pltpu
from jax.sharding import PartitionSpec as P

CSPLIT = 8
CLIP_NORM = 40.0
NOISE_STD = 0.4
GATHER_LIMIT = 16 << 20
CHUNKS = 4
BLOCKS_PER_DOT = 8
MESH = pl.DeviceIdType.MESH


def head_kernel(n_dp, n_cls, feat_ref, weight_ref, side_ref, rows_ref, coef_ref,
                feats, wcols, exps, coefs, sides, lanes, labels, stats, all_stats, maxima, energies, scales,
                send_sem, sib_send_sem, recv_sem, sib_recv_sem, wsend_sem, wrecv_sem,
                ssend_sem, srecv_sem, tsend_sem, trecv_sem, local_sem, rows_sem, coef_sem):
    me = lax.axis_index("dp")
    cls = lax.axis_index("cls")
    core = cls % 2
    sibling = cls + 1 - 2 * core
    stages = n_dp.bit_length() - 1
    rows, depth = feat_ref.shape
    half = rows // 2
    chunks, _, depth_block, width = wcols.shape
    cols = chunks * width
    padded = lanes.shape[1]
    row_block = rows_ref.shape[2]
    per = BLOCKS_PER_DOT
    count = CSPLIT * n_cls
    place = me % CSPLIT * n_cls + cls

    def group_peer(hop):
        spot = (place + hop) % count
        return (me // CSPLIT * CSPLIT + spot // n_cls, spot % n_cls)

    barrier = pltpu.get_barrier_semaphore()
    for hop in range(1, n_dp):
        pl.semaphore_signal(barrier, inc=1, device_id=((me + hop) % n_dp, cls), device_id_type=MESH)
    for hop in range(1, count):
        pl.semaphore_signal(barrier, inc=1, device_id=group_peer(hop), device_id_type=MESH)
    pl.semaphore_wait(barrier, n_dp - 1 + count - 1)

    bit_step = [(1 << b) * (1 - 2 * ((me // (1 << b)) % 2)) for b in range(stages)]

    def stage_steps(which):
        table = [bit_step[b] for b in range(stages - 1, 1, -1)]
        return table + [bit_step[1] * (1 - which) + bit_step[0] * which,
                        bit_step[0] * (1 - which) + bit_step[1] * which]

    steps = stage_steps(core)
    sib_steps = stage_steps(1 - core)

    def origin(mask, table):
        spot = me
        for s in range(stages):
            if mask >> s & 1:
                spot = spot + table[s]
        return spot

    mine = pl.ds(pl.multiple_of(core * half, half), half)
    other = pl.ds(pl.multiple_of((1 - core) * half, half), half)
    sends = []

    def push(source, target, out_sem, in_sem, device):
        copy = pltpu.make_async_remote_copy(
            src_ref=source, dst_ref=target, send_sem=out_sem, recv_sem=in_sem,
            device_id=device, device_id_type=MESH,
        )
        copy.start()
        sends.append(copy)

    def arrived(ref, sem):
        pltpu.make_async_remote_copy(
            src_ref=ref, dst_ref=ref, send_sem=sem, recv_sem=sem,
            device_id=(me, sibling), device_id_type=MESH,
        ).wait_recv()

    def forward(mask, source, slot):
        for s in range(mask.bit_length(), stages):
            push(source, feats.at[slot, mine], send_sem.at[mask * stages + s],
                 recv_sem.at[mask | 1 << s], (me + steps[s], cls))
        if mask:
            push(source, feats.at[slot, mine], sib_send_sem.at[mask], sib_recv_sem.at[mask], (me, sibling))

    def send_chunk(c):
        for hop in range(1, n_dp):
            peer = (me + hop) % n_dp
            first = pl.multiple_of(peer % CSPLIT * cols + c * width, width)
            push(weight_ref.at[:, pl.ds(first, width)], wcols.at[c, me],
                 wsend_sem.at[c * n_dp + hop], wrecv_sem.at[c * n_dp + hop], (peer, cls))

    forward(0, feat_ref.at[mine], me)
    keep = [
        pltpu.make_async_copy(feat_ref, feats.at[me], local_sem.at[0]),
        pltpu.make_async_copy(side_ref, sides.at[me], local_sem.at[1]),
    ] + [
        pltpu.make_async_copy(
            weight_ref.at[:, pl.ds(pl.multiple_of(me % CSPLIT * cols + c * width, width), width)],
            wcols.at[c, me], local_sem.at[2 + c])
        for c in range(chunks)
    ]
    for copy in keep:
        copy.start()
    for hop in range(1, n_dp):
        push(side_ref, sides.at[me], ssend_sem.at[hop], srecv_sem.at[hop], ((me + hop) % n_dp, cls))

    for hop in range(1, n_dp):
        arrived(sides.at[(me + n_dp - hop) % n_dp], srecv_sem.at[hop])
    for copy in keep:
        copy.wait()
    fill = jnp.zeros((128 - sides.shape[1], padded), jnp.float32)
    lanes[...] = jnp.zeros_like(lanes)

    def spread_labels(i, carry):
        labels[i] = jnp.concatenate([sides[i], fill], axis=0).T
        return carry

    lax.fori_loop(0, n_dp, spread_labels, 0)
    for i in range(n_dp):
        energies[i:i + 1, :] = sides[i, 1:2, :]

    for mask in range(1, n_dp):
        slot = origin(mask, steps)
        arrived(feats.at[slot, mine], recv_sem.at[mask])
        forward(mask, feats.at[slot, mine], slot)
        if mask % (n_dp // chunks) == 1:
            send_chunk(mask // (n_dp // chunks))
    for mask in range(1, n_dp):
        arrived(feats.at[origin(mask, sib_steps), other], sib_recv_sem.at[mask])

    first_row = pl.multiple_of(me // CSPLIT * row_block, row_block)
    row_copies = [
        pltpu.make_async_copy(feats.at[i, :, pl.ds(first_row, row_block)], rows_ref.at[i], rows_sem.at[i])
        for i in range(n_dp)
    ]
    for copy in row_copies:
        copy.start()

    base = cls * (CSPLIT * cols) + me % CSPLIT * cols

    def hits(block_labels, c, shape):
        offset = block_labels.astype(jnp.int32) - (base + c * width)
        return lax.broadcasted_iota(jnp.int32, shape, 1) == offset

    def chunk_body(c, carry):
        for hop in range(1, n_dp):
            arrived(wcols.at[c, (me + n_dp - hop) % n_dp], wrecv_sem.at[c * n_dp + hop])

        def group_body(g, inner):
            blocks = pl.ds(g * per, per)
            logits = jnp.dot(
                feats[blocks].reshape(per * rows, depth), wcols[c].reshape(depth, width),
                preferred_element_type=jnp.float32)
            hit = hits(labels[blocks, 0:rows, 0:1].reshape(per * rows, 1), c, logits.shape)
            top = jnp.max(logits, axis=1, keepdims=True)
            exponent = jnp.exp(logits - top)
            total = jnp.sum(exponent, axis=1, keepdims=True)
            square = jnp.sum(exponent * exponent, axis=1, keepdims=True)
            picked = jnp.sum(jnp.where(hit, logits, 0.0), axis=1, keepdims=True)
            exps[c, blocks] = exponent.reshape(per, rows, width)
            held = lanes[blocks, 0:rows, :].reshape(per * rows, 128)
            lane = lax.broadcasted_iota(jnp.int32, held.shape, 1) - 4 * c
            held = jnp.where(lane == 0, top, held)
            held = jnp.where(lane == 1, total, held)
            held = jnp.where(lane == 2, square, held)
            held = jnp.where(lane == 3, picked, held)
            lanes[blocks, 0:rows, :] = held.reshape(per, rows, 128)
            return inner

        return lax.fori_loop(0, n_dp // per, group_body, carry)

    lax.fori_loop(0, chunks, chunk_body, 0)

    for i in range(n_dp):
        turned = lanes[i].T
        tops = [turned[4 * c:4 * c + 1] for c in range(chunks)]
        top = functools.reduce(jnp.maximum, tops)
        fades = [jnp.exp(t - top) for t in tops]
        stats[0, i:i + 1, :] = top
        stats[1, i:i + 1, :] = sum(turned[4 * c + 1:4 * c + 2] * fades[c] for c in range(chunks))
        stats[2, i:i + 1, :] = sum(turned[4 * c + 2:4 * c + 3] * fades[c] * fades[c] for c in range(chunks))
        stats[3, i:i + 1, :] = sum(turned[4 * c + 3:4 * c + 4] for c in range(chunks))
        for c in range(chunks):
            maxima[c, i:i + 1, :] = tops[c]

    for hop in range(1, count):
        push(stats, all_stats.at[place], tsend_sem.at[hop], trecv_sem.at[hop], group_peer(hop))
    all_stats[pl.ds(place, 1)] = stats[...][None]
    for hop in range(1, count):
        arrived(all_stats.at[(place + count - hop) % count], trecv_sem.at[hop])

    row_max = all_stats[0, 0]
    for d in range(1, count):
        row_max = jnp.maximum(row_max, all_stats[d, 0])
    row_total = jnp.zeros_like(row_max)
    row_square = jnp.zeros_like(row_max)
    picked = jnp.zeros_like(row_max)
    for d in range(count):
        fade = jnp.exp(all_stats[d, 0] - row_max)
        row_total = row_total + all_stats[d, 1] * fade
        row_square = row_square + all_stats[d, 2] * fade * fade
        picked = picked + all_stats[d, 3]
    spread = row_square / (row_total * row_total) - 2.0 * jnp.exp(picked - row_max) / row_total + 1.0
    factor = CLIP_NORM * lax.rsqrt(jnp.maximum(energies[...] * spread, CLIP_NORM * CLIP_NORM))
    scales[chunks] = factor
    for c in range(chunks):
        scales[c] = factor * (jnp.exp(maxima[c] - row_max) / row_total)
    for i in range(n_dp):
        for c in range(chunks + 1):
            sides[i, c:c + 1, :] = scales[c, i:i + 1, :]

    def coef_copy(i):
        return pltpu.make_async_copy(coefs.at[i], coef_ref.at[i], coef_sem.at[i])

    def coef_body(i, carry):
        columns = jnp.concatenate([sides[i], fill], axis=0).T[0:rows]
        block_labels = labels[i, 0:rows, 0:1]
        for c in range(chunks):
            hit = hits(block_labels, c, (rows, width))
            value = exps[c, i] * columns[:, c:c + 1] - jnp.where(hit, columns[:, chunks:chunks + 1], 0.0)
            coefs[i, :, c * width:(c + 1) * width] = value.astype(coefs.dtype)
        coef_copy(i).start()
        return carry

    lax.fori_loop(0, n_dp, coef_body, 0)
    for i in range(n_dp):
        coef_copy(i).wait()
        row_copies[i].wait()
    for copy in sends:
        copy.wait_send()


def head(features, weight, side, n_dp, n_cls, row_block, col_block):
    stages = n_dp.bit_length() - 1
    rows, depth = features.shape
    padded = side.shape[1]
    count = CSPLIT * n_cls
    width = col_block // CHUNKS
    anywhere = pl.BlockSpec(memory_space=pl.ANY)
    dma = pltpu.SemaphoreType.DMA
    f32 = jnp.float32
    return pl.pallas_call(
        functools.partial(head_kernel, n_dp, n_cls),
        out_shape=(
            jax.ShapeDtypeStruct((n_dp, rows, row_block), features.dtype),
            jax.ShapeDtypeStruct((n_dp, rows, col_block), jnp.bfloat16),
        ),
        in_specs=[anywhere] * 3,
        out_specs=(anywhere,) * 2,
        scratch_shapes=[
            pltpu.VMEM((n_dp, rows, depth), features.dtype),
            pltpu.VMEM((CHUNKS, n_dp, weight.shape[0], width), weight.dtype),
            pltpu.VMEM((CHUNKS, n_dp, rows, width), f32),
            pltpu.VMEM((n_dp, rows, col_block), jnp.bfloat16),
            pltpu.VMEM((n_dp,) + side.shape, f32),
            pltpu.VMEM((n_dp, padded, 128), f32),
            pltpu.VMEM((n_dp, padded, 128), f32),
            pltpu.VMEM((4, n_dp, padded), f32),
            pltpu.VMEM((count, 4, n_dp, padded), f32),
            pltpu.VMEM((CHUNKS, n_dp, padded), f32),
            pltpu.VMEM((n_dp, padded), f32),
            pltpu.VMEM((CHUNKS + 1, n_dp, padded), f32),
            dma((n_dp * stages,)), dma((n_dp,)), dma((n_dp,)), dma((n_dp,)),
            dma((CHUNKS * n_dp,)), dma((CHUNKS * n_dp,)),
            dma((n_dp,)), dma((n_dp,)), dma((count,)), dma((count,)),
            dma((2 + CHUNKS,)), dma((n_dp,)), dma((n_dp,)),
        ],
        compiler_params=pltpu.CompilerParams(
            collective_id=0, has_side_effects=True, vmem_limit_bytes=60 << 20),
    )(features, weight, side)


def examples_split(features, labels, weight, noise):
    tok_rows = features.shape[0]
    feature_dim = features.shape[1]
    class_shard = weight.shape[1]
    groups = lax.axis_size("dp") // CSPLIT
    row_block = feature_dim // groups
    col_block = class_shard // CSPLIT
    slot_count = groups * CSPLIT
    feature_slots = jnp.broadcast_to(
        features.reshape(tok_rows, groups, 1, row_block), (tok_rows, groups, CSPLIT, row_block)
    ).reshape(tok_rows, slot_count, row_block)
    logits = jnp.dot(
        features,
        lax.all_gather(weight, "dp", axis=0, tiled=True),
        preferred_element_type=jnp.float32,
    )
    offset = labels - lax.axis_index("cls") * class_shard
    label_hit = lax.broadcasted_iota(jnp.int32, (tok_rows, class_shard), 1) == offset[:, None]
    onehot = label_hit.astype(jnp.float32)
    local_max = jnp.max(logits, axis=1)
    exponent = jnp.exp(logits - local_max[:, None])
    row_total = jnp.sum(exponent, axis=1)
    row_square = jnp.sum(exponent * exponent, axis=1)
    picked = jnp.sum(onehot * logits, axis=1)
    global_max = lax.pmax(local_max, "cls")
    rescale = jnp.exp(local_max - global_max)
    row_total, row_square, picked = lax.psum(
        (row_total * rescale, row_square * rescale * rescale, picked), "cls"
    )
    softmax = exponent * (jnp.exp(local_max - global_max) / row_total)[:, None]
    label_prob = jnp.exp(picked - global_max) / row_total
    spread = row_square / (row_total * row_total) - 2.0 * label_prob + 1.0
    energy = jnp.sum(jnp.square(features.astype(jnp.float32)), axis=1)
    factor = CLIP_NORM * lax.rsqrt(jnp.maximum(energy * spread, CLIP_NORM * CLIP_NORM))
    weighted = (factor[:, None] * (softmax - onehot)).astype(jnp.bfloat16)
    coef_slots = jnp.broadcast_to(
        weighted.reshape(tok_rows, 1, CSPLIT, col_block), (tok_rows, groups, CSPLIT, col_block)
    ).reshape(tok_rows, slot_count, col_block)
    feature_recv, coef_recv = (
        lax.all_to_all(feature_slots, "dp", split_axis=1, concat_axis=1, tiled=True),
        lax.all_to_all(coef_slots, "dp", split_axis=1, concat_axis=1, tiled=True),
    )
    grad_block = lax.dot_general(
        feature_recv, coef_recv, (((0, 1), (0, 1)), ((), ())), preferred_element_type=jnp.float32
    )
    return (grad_block + NOISE_STD * noise[0, 0]).reshape(noise.shape)


def on_device(features, labels, weight, noise):
    n_dp = lax.axis_size("dp")
    if n_dp * features.size * features.dtype.itemsize > GATHER_LIMIT:
        return examples_split(features, labels, weight, noise)
    feature_dim = features.shape[1]
    class_shard = weight.shape[1]
    groups = n_dp // CSPLIT
    row_block = feature_dim // groups
    col_block = class_shard // CSPLIT
    padded = -(-features.shape[0] // 128) * 128
    own_energy = jnp.sum(jnp.square(features.astype(jnp.float32)), axis=1)
    side = jnp.pad(
        jnp.stack([labels.astype(jnp.float32), own_energy]), ((0, 6), (0, padded - features.shape[0])))
    rows, coef = head(features, weight, side, n_dp, lax.axis_size("cls"), row_block, col_block)
    grad = lax.dot_general(rows, coef, (((0, 1), (0, 1)), ((), ())), preferred_element_type=jnp.float32)
    return (grad + NOISE_STD * noise[0, 0]).reshape(noise.shape)


def solution(mesh):
    placed = (P("dp", None), P("dp"), P("dp", "cls"), P("dp", "cls", None, None))
    return jax.shard_map(
        on_device, mesh=mesh, in_specs=placed, out_specs=P("dp", "cls", None, None), check_vma=False
    )
```
